128 devices in a mesh: node: 32 (over x, y, core), local: 4 (over z).
Axes of the slice: x: 4, y: 4, z: 4, core: 2. Of those that a mesh axis runs over, the one named last changes fastest.
Arguments:
- tokens_in: bfloat16 [16384, 3584], P(('node', 'local')), may hold values from -6 to 6
- grad_out: bfloat16 [16384, 3584], P(('node', 'local')), may hold values from -6 to 6
- expert_ids: int32 [16384, 3], P(('node', 'local')), may hold values from 0 to 127, as said below
- gate_weights: float32 [16384, 3], P(('node', 'local')), may hold values from 0.2 to 1
- w_gate: bfloat16 [128, 3584, 1024], P(('node', 'local')), may hold values from -0.09375 to 0.09375
- w_up: bfloat16 [128, 3584, 1024], P(('node', 'local')), may hold values from -0.09375 to 0.09375
- w_down: bfloat16 [128, 1024, 3584], P(('node', 'local')), may hold values from -0.09375 to 0.09375
Outputs:
- grad_in: bfloat16 [16384, 3584], P(('node', 'local'))
The draws below stay inside these ranges and needn't reach their ends.
Inputs may be any that keep to these rules, and one draw needn't show every extreme that they name: `expert_ids`: each row names 3 different experts. Among the 128 tokens of one device no expert is named more than 6 times, and one expert is named exactly 6 times by the tokens of every device.
All inputs are finite; a program needn't handle non-finite values.
Results may differ from the reference program's by a relative error of at most 0.0058.
Values may be sent and summed in bfloat16 or wider, within the bound.
No kernel may reach another device: no remote copies, remote signals or barrier semaphores. Data moves between devices by JAX's collectives and lax.ppermute only.
A program may use at most 128 MiB of HBM per device.

```python
import jax
import jax.numpy as jnp
from jax import lax

D = 3584
FF = 1024
TOPK = 3
TOK_DEV = 128
EXPERTS = 128
TOKENS = 16384
CAP = 6
N_NODE = 32
N_LOCAL = 4


def draw_expert_ids(key, part):
    blocks = TOKENS // TOK_DEV
    picks = TOK_DEV * TOPK
    mean_load = picks // EXPERTS
    popular = jax.random.permutation(jax.random.fold_in(key, 1), EXPERTS).astype(jnp.int32)
    shifts = jax.random.randint(jax.random.fold_in(key, 2), (blocks, EXPERTS // 2), 0, mean_load + 1)
    shifts = shifts.at[:, 0].set(mean_load)
    loads = jnp.stack([mean_load + shifts, mean_load - shifts], axis=2).reshape(blocks, EXPERTS)
    ends = jnp.cumsum(loads, axis=1)
    position = jnp.arange(picks, dtype=jnp.int32)
    ranks = jnp.sum((ends[:, None, :] <= position[None, :, None]).astype(jnp.int32), axis=2)
    sequence = popular[ranks]
    row_keys = jax.random.split(jax.random.fold_in(key, 3), blocks)
    orders = jax.vmap(lambda one_key: jax.random.permutation(one_key, TOK_DEV))(row_keys)
    inverse = jnp.argsort(orders, axis=1).astype(jnp.int32)
    index = inverse[:, :, None] + TOK_DEV * jnp.arange(TOPK, dtype=jnp.int32)[None, None, :]
    chosen = jnp.take_along_axis(sequence, index.reshape(blocks, picks), axis=1)
    return chosen.reshape(TOKENS, TOPK).astype(jnp.int32)


def level_of(rng, extent, pieces, smallest, high):
    def one(dim, shards_of):
        steps = jax.random.uniform(jax.random.fold_in(jax.random.fold_in(rng, 6), dim), (shards_of,), jnp.float32, smallest / len(pieces), high / len(pieces))
        return jnp.repeat(jnp.exp(steps), extent[dim] // shards_of).reshape((-1,) + (1,) * (len(extent) - dim - 1))

    factor_of = one(*pieces[0])
    for cut in pieces[1:]:
        factor_of = factor_of * one(*cut)
    return factor_of


def gaussian(key, dims, width, reach, shards=(), held_as=jnp.bfloat16):
    entries = jax.random.normal(key, dims, jnp.float32) * width
    if len(shards) > 0:
        entries = level_of(key, dims, shards, -0.22, 0.18) * entries
    return jnp.clip(entries, min=-reach, max=reach).astype(held_as)


def setup_inputs(seed: int = 0) -> dict:
    keys = jax.random.split(jax.random.key(seed), 8)
    tokens_in = gaussian(keys[0], (TOKENS, D), 1.0, 6.0, ((0, 128),))
    grad_out = gaussian(keys[1], (TOKENS, D), 1.0, 6.0, ((0, 128),))
    expert_ids = draw_expert_ids(jax.random.fold_in(keys[7], 71), 0)
    gate_weights = jnp.clip(0.2 + 0.8 * jax.random.uniform(keys[3], (TOKENS, TOPK), jnp.float32) ** level_of(keys[3], (TOKENS, TOPK), ((0, 128),), -0.2, 0.2), 0.2, 1.0)
    w_gate = gaussian(keys[4], (EXPERTS, D, FF), D ** -0.5, 0.09375, ((0, 128),))
    w_up = gaussian(keys[5], (EXPERTS, D, FF), D ** -0.5, 0.09375, ((0, 128),))
    w_down = gaussian(keys[6], (EXPERTS, FF, D), D ** -0.5, 0.09375, ((0, 128),))
    return dict(tokens_in=tokens_in, grad_out=grad_out, expert_ids=expert_ids, gate_weights=gate_weights, w_gate=w_gate, w_up=w_up, w_down=w_down)


def expert_grads(rows_x, rows_y, w_gate, w_up, w_down):
    gate_pre = jnp.dot(rows_x, w_gate, preferred_element_type=jnp.float32)
    up_pre = jnp.dot(rows_x, w_up, preferred_element_type=jnp.float32)
    back_hidden = lax.dot_general(rows_y, w_down, (((1,), (1,)), ((), ())), preferred_element_type=jnp.float32)
    sig = jax.nn.sigmoid(gate_pre)
    d_gate = (back_hidden * up_pre * sig * (1.0 + gate_pre * (1.0 - sig))).astype(jnp.bfloat16)
    d_up = (back_hidden * gate_pre * sig).astype(jnp.bfloat16)
    first = lax.dot_general(d_gate, w_gate, (((1,), (1,)), ((), ())), preferred_element_type=jnp.float32)
    second = lax.dot_general(d_up, w_up, (((1,), (1,)), ((), ())), preferred_element_type=jnp.float32)
    return first + second


def reference(tokens_in, grad_out, expert_ids, gate_weights, w_gate, w_up, w_down):
    devices = N_NODE * N_LOCAL
    picks = TOK_DEV * TOPK
    blocks = expert_ids.reshape(devices, picks)
    onehot = (blocks[:, :, None] == jnp.arange(EXPERTS, dtype=jnp.int32)[None, None, :]).astype(jnp.int32)
    slot = jnp.sum((jnp.cumsum(onehot, axis=1) - onehot) * onehot, axis=2)
    source = jnp.arange(devices, dtype=jnp.int32)[:, None]
    position = (blocks * (devices * CAP) + source * CAP + slot).astype(jnp.int32)
    flat_index = jnp.arange(devices * picks, dtype=jnp.int32).reshape(devices, picks)
    table = jnp.full((EXPERTS * devices * CAP,), devices * picks, dtype=jnp.int32)
    table = table.at[position.reshape(-1)].set(flat_index.reshape(-1)).reshape(EXPERTS, devices * CAP)
    x_pad = jnp.concatenate([tokens_in, jnp.zeros((1, D), tokens_in.dtype)], axis=0)
    y_pad = jnp.concatenate([grad_out, jnp.zeros((1, D), grad_out.dtype)], axis=0)
    gate_flat = jnp.concatenate([gate_weights.reshape(-1), jnp.zeros((1,), gate_weights.dtype)], axis=0)

    def visit(total, inputs):
        index, one_gate, one_up, one_down = inputs
        token = (index // TOPK).astype(jnp.int32)
        part = expert_grads(x_pad[token], y_pad[token], one_gate, one_up, one_down).astype(jnp.bfloat16)
        total = total.at[token].add(gate_flat[index][:, None] * part.astype(jnp.float32), mode="drop")
        return total, None

    total, unused = lax.scan(visit, jnp.zeros((TOKENS, D), jnp.float32), (table, w_gate, w_up, w_down))
    return total.astype(jnp.bfloat16)
```

```python
import functools

import jax
import jax.numpy as jnp
from jax import lax
from jax.experimental import pallas as pl
from jax.experimental.pallas import tpu as pltpu
from jax.sharding import PartitionSpec as P

AXES = ("node", "local")
CHUNKS = ((0, 4), (4, 2))
VMEM_LIMIT = 60 * 1024 * 1024


def params():
    return pltpu.CompilerParams(dimension_semantics=("arbitrary",), vmem_limit_bytes=VMEM_LIMIT)


def pack_body(slot_ref, x_ref, y_ref, out_ref, pick_ref, *, first, count, half):
    step = pl.program_id(0)
    experts, tok_rows = slot_ref.shape

    @pl.when(step == 0)
    def _():
        shape = (experts, count, tok_rows)
        wanted = first + lax.broadcasted_iota(jnp.int32, shape, 1)
        slots = jnp.broadcast_to(slot_ref[...][:, None, :], shape)
        picked = jnp.where(slots == wanted, 1.0, 0.0)
        pick_ref[...] = picked.reshape(experts * count, tok_rows).astype(jnp.bfloat16)

    def emit(rows):
        block = jnp.dot(pick_ref[...], rows, preferred_element_type=jnp.float32)
        out_ref[...] = block.astype(jnp.bfloat16).reshape(out_ref.shape)

    @pl.when(step < half)
    def _():
        emit(x_ref[...])

    @pl.when(step >= half)
    def _():
        emit(y_ref[...])


def pack(slot_by_expert, x, y, first, count, block=896):
    experts, tok_rows = slot_by_expert.shape
    width = x.shape[1]
    half = width // block
    return pl.pallas_call(
        functools.partial(pack_body, first=first, count=count, half=half),
        grid=(2 * half,),
        in_specs=[
            pl.BlockSpec((experts, tok_rows), lambda j: (0, 0)),
            pl.BlockSpec((tok_rows, block), lambda j: (0, jnp.minimum(j, half - 1))),
            pl.BlockSpec((tok_rows, block), lambda j: (0, jnp.maximum(j - half, 0))),
        ],
        out_specs=pl.BlockSpec((experts, count, block), lambda j: (0, 0, j)),
        out_shape=jax.ShapeDtypeStruct((experts, count, 2 * width), jnp.bfloat16),
        scratch_shapes=[pltpu.VMEM((experts * count, tok_rows), jnp.bfloat16)],
        compiler_params=params(),
        name="pack",
    )(slot_by_expert, x, y)


def expert_body(
    x_ref, y_ref, gate_ref, up_ref, down_ref, out_ref,
    gate_acc, up_acc, back_acc, d_gate_ref, d_up_ref, *, steps,
):
    step = pl.program_id(0)
    rows = gate_acc.shape[0]
    block = x_ref.shape[2]
    across = (((1,), (1,)), ((), ()))

    def add(acc, value, start):
        if start:
            acc[...] = value
        else:
            acc[...] += value

    def forward(start):
        x = x_ref[...].reshape(rows, block)
        y = y_ref[...].reshape(rows, block)
        add(gate_acc, jnp.dot(x, gate_ref[...], preferred_element_type=jnp.float32), start)
        add(up_acc, jnp.dot(x, up_ref[...], preferred_element_type=jnp.float32), start)
        add(back_acc, lax.dot_general(y, down_ref[...], across, preferred_element_type=jnp.float32), start)

    @pl.when(step == 0)
    def _():
        forward(True)

    @pl.when((step > 0) & (step < steps))
    def _():
        forward(False)

    @pl.when(step == steps - 1)
    def _():
        gate_pre = gate_acc[...]
        up_pre = up_acc[...]
        back = back_acc[...]
        sig = 1.0 / (1.0 + jnp.exp(-gate_pre))
        d_gate_ref[...] = (back * up_pre * sig * (1.0 + gate_pre * (1.0 - sig))).astype(jnp.bfloat16)
        d_up_ref[...] = (back * gate_pre * sig).astype(jnp.bfloat16)

    @pl.when(step >= steps)
    def _():
        total = lax.dot_general(d_gate_ref[...], gate_ref[...], across, preferred_element_type=jnp.float32)
        total += lax.dot_general(d_up_ref[...], up_ref[...], across, preferred_element_type=jnp.float32)
        out_ref[...] = total.astype(jnp.bfloat16).reshape(out_ref.shape)


def expert(arrived, w_gate, w_up, w_down, block=512):
    sources, count, double = arrived.shape
    width = double // 2
    hidden = w_gate.shape[1]
    rows = sources * count
    steps = width // block
    there = lambda j: jnp.minimum(j, steps - 1)
    back = lambda j: jnp.where(j < steps, j, 2 * steps - 1 - j)
    return pl.pallas_call(
        functools.partial(expert_body, steps=steps),
        grid=(2 * steps,),
        in_specs=[
            pl.BlockSpec((sources, count, block), lambda j: (0, 0, there(j))),
            pl.BlockSpec((sources, count, block), lambda j: (0, 0, steps + there(j))),
            pl.BlockSpec((block, hidden), lambda j: (back(j), 0)),
            pl.BlockSpec((block, hidden), lambda j: (back(j), 0)),
            pl.BlockSpec((hidden, block), lambda j: (0, there(j))),
        ],
        out_specs=pl.BlockSpec(
            (sources, count, block), lambda j: (0, 0, jnp.where(j < steps, steps - 1, 2 * steps - 1 - j))
        ),
        out_shape=jax.ShapeDtypeStruct((sources, count, width), jnp.bfloat16),
        scratch_shapes=[pltpu.VMEM((rows, hidden), jnp.float32)] * 3
        + [pltpu.VMEM((rows, hidden), jnp.bfloat16)] * 2,
        compiler_params=params(),
        cost_estimate=pl.CostEstimate(
            flops=10 * rows * width * hidden,
            transcendentals=rows * hidden,
            bytes_accessed=2 * (5 * width * hidden + 3 * rows * width),
        ),
        name="expert",
    )(arrived, arrived, w_gate, w_up, w_down)


def combine_body(slot_ref, weight_ref, block_ref, *refs, first, count, last):
    prior_ref, out_ref, scale_ref = (refs if last else (None,) + refs)
    tok_rows, experts = slot_ref.shape
    wide = experts * count

    @pl.when(pl.program_id(0) == 0)
    def _():
        for j in range(count):
            scale = jnp.where(slot_ref[...] == first + j, weight_ref[...], 0.0)
            high = scale.astype(jnp.bfloat16)
            low = (scale - high.astype(jnp.float32)).astype(jnp.bfloat16)
            scale_ref[j, 0:tok_rows, :] = high
            scale_ref[j, tok_rows : 2 * tok_rows, :] = low

    total = jnp.zeros((2 * tok_rows, block_ref.shape[2]), jnp.float32)
    for j in range(count):
        total += jnp.dot(scale_ref[j], block_ref[:, j, :], preferred_element_type=jnp.float32)
    total = total[0:tok_rows] + total[tok_rows : 2 * tok_rows]
    if last:
        total = total + prior_ref[...]
    out_ref[...] = total.astype(out_ref.dtype)


def combine(slot, weight, returned, prior, first, count, block=896):
    tok_rows, experts = slot.shape
    width = returned.shape[2]
    last = prior is not None
    whole = pl.BlockSpec((tok_rows, experts), lambda j: (0, 0))
    part = pl.BlockSpec((tok_rows, block), lambda j: (0, j))
    operands = (slot, weight, returned) + ((prior,) if last else ())
    return pl.pallas_call(
        functools.partial(combine_body, first=first, count=count, last=last),
        grid=(width // block,),
        in_specs=[whole, whole, pl.BlockSpec((experts, count, block), lambda j: (0, 0, j))]
        + ([part] if last else []),
        out_specs=part,
        out_shape=jax.ShapeDtypeStruct((tok_rows, width), jnp.bfloat16 if last else jnp.float32),
        scratch_shapes=[pltpu.VMEM((count, 2 * tok_rows, experts), jnp.bfloat16)],
        compiler_params=params(),
        name="combine",
    )(*operands)


def exchange(block):
    return lax.all_to_all(block, AXES, split_axis=0, concat_axis=0, tiled=True)


def body(tokens_in, grad_out, expert_ids, gate_weights, w_gate, w_up, w_down):
    tok_rows = tokens_in.shape[0]
    experts = lax.axis_size("node") * lax.axis_size("local")
    numbers = jnp.arange(experts, dtype=jnp.int32)
    named = expert_ids[:, :, None] == numbers[None, None, :]
    member = jnp.any(named, axis=1)
    weight = jnp.sum(jnp.where(named, gate_weights[:, :, None], 0.0), axis=1)
    order = jnp.arange(tok_rows, dtype=jnp.int32)
    earlier = (order[:, None] > order[None, :]).astype(jnp.bfloat16)
    slot = jnp.dot(earlier, member.astype(jnp.bfloat16), preferred_element_type=jnp.float32)
    slot = jnp.where(member, slot, -1.0).astype(jnp.int32)
    slot_by_expert = slot.T
    (first_a, count_a), (first_b, count_b) = CHUNKS
    payload_a = pack(slot_by_expert, tokens_in, grad_out, first_a, count_a)
    payload_a, slot_late = lax.optimization_barrier((payload_a, slot_by_expert))
    arrived_a = exchange(payload_a)
    payload_b = pack(slot_late, tokens_in, grad_out, first_b, count_b)
    arrived_b = exchange(payload_b)
    result_a = expert(arrived_a, w_gate[0], w_up[0], w_down[0])
    returned_a = exchange(result_a)
    result_b = expert(arrived_b, w_gate[0], w_up[0], w_down[0])
    returned_b = exchange(result_b)
    total = combine(slot, weight, returned_a, None, first_a, count_a)
    return combine(slot, weight, returned_b, total, first_b, count_b)


def solution(mesh):
    rows = P(AXES, None)
    cube = P(AXES, None, None)
    in_specs = (rows, rows, rows, rows, cube, cube, cube)
    return jax.shard_map(body, mesh=mesh, in_specs=in_specs, out_specs=rows, check_vma=False)
```

```python
import functools

import jax
import jax.numpy as jnp
from jax import lax
from jax.experimental import pallas as pl
from jax.experimental.pallas import tpu as pltpu
from jax.sharding import PartitionSpec as P

AXES = ("node", "local")
CHUNKS = ((0, 4), (4, 2))
VMEM_LIMIT = 60 * 1024 * 1024
ACROSS = (((1,), (1,)), ((), ()))


def params():
    return pltpu.CompilerParams(dimension_semantics=("arbitrary",), vmem_limit_bytes=VMEM_LIMIT)


def slots_of(ids_ref, experts):
    topk, tok_rows = ids_ref.shape
    numbers = lax.broadcasted_iota(jnp.int32, (experts, tok_rows), 0)
    member = ids_ref[0:1, :] == numbers
    for k in range(1, topk):
        member = member | (ids_ref[k : k + 1, :] == numbers)
    source = lax.broadcasted_iota(jnp.int32, (tok_rows, tok_rows), 0)
    target = lax.broadcasted_iota(jnp.int32, (tok_rows, tok_rows), 1)
    before = jnp.where(source < target, 1.0, 0.0).astype(jnp.bfloat16)
    flags = jnp.where(member, 1.0, 0.0).astype(jnp.bfloat16)
    slot = jnp.dot(flags, before, preferred_element_type=jnp.float32)
    return jnp.where(member, slot, -1.0)


def pack_body(ids_ref, x_ref, y_ref, out_ref, pick_ref, *, first, count, experts):
    tok_rows = ids_ref.shape[1]

    @pl.when(pl.program_id(0) == 0)
    def _():
        shape = (experts, 2 * count, 2 * tok_rows)
        slot = slots_of(ids_ref, experts)
        slot = jnp.concatenate([slot, slot], axis=1)
        row = lax.broadcasted_iota(jnp.int32, shape, 1)
        column = lax.broadcasted_iota(jnp.int32, shape, 2)
        wanted = (first + row % count).astype(jnp.float32)
        same = (row >= count) == (column >= tok_rows)
        hit = same & (jnp.broadcast_to(slot[:, None, :], shape) == wanted)
        picked = jnp.where(hit, 1.0, 0.0)
        pick_ref[...] = picked.reshape(experts * 2 * count, 2 * tok_rows).astype(jnp.bfloat16)

    both = jnp.concatenate([x_ref[...], y_ref[...]], axis=0)
    block = jnp.dot(pick_ref[...], both, preferred_element_type=jnp.float32)
    out_ref[...] = block.astype(jnp.bfloat16).reshape(out_ref.shape)


def pack(ids, x, y, experts, first, count, block=1792):
    topk, tok_rows = ids.shape
    width = x.shape[1]
    part = pl.BlockSpec((tok_rows, block), lambda j: (0, j))
    return pl.pallas_call(
        functools.partial(pack_body, first=first, count=count, experts=experts),
        grid=(width // block,),
        in_specs=[pl.BlockSpec((topk, tok_rows), lambda j: (0, 0)), part, part],
        out_specs=pl.BlockSpec((experts, 2 * count, block), lambda j: (0, 0, j)),
        out_shape=jax.ShapeDtypeStruct((experts, 2 * count, width), jnp.bfloat16),
        scratch_shapes=[pltpu.VMEM((experts * 2 * count, 2 * tok_rows), jnp.bfloat16)],
        compiler_params=params(),
        name="pack",
    )(ids, x, y)


def expert_body(
    in_ref, gate_ref, up_ref, down_ref, out_ref,
    gate_acc, up_acc, back_acc, d_gate_ref, d_up_ref, *, steps,
):
    step = pl.program_id(0)
    rows = gate_acc.shape[0]
    count = in_ref.shape[1] // 2
    block = in_ref.shape[2]

    def add(acc, value, start):
        if start:
            acc[...] = value
        else:
            acc[...] += value

    def forward(start):
        x = in_ref[:, 0:count, :].reshape(rows, block)
        y = in_ref[:, count : 2 * count, :].reshape(rows, block)
        add(gate_acc, jnp.dot(x, gate_ref[...], preferred_element_type=jnp.float32), start)
        add(up_acc, jnp.dot(x, up_ref[...], preferred_element_type=jnp.float32), start)
        add(back_acc, lax.dot_general(y, down_ref[...], ACROSS, preferred_element_type=jnp.float32), start)

    @pl.when(step == 0)
    def _():
        forward(True)

    @pl.when((step > 0) & (step < steps))
    def _():
        forward(False)

    @pl.when(step == steps - 1)
    def _():
        gate_pre = gate_acc[...]
        up_pre = up_acc[...]
        back = back_acc[...]
        sig = 1.0 / (1.0 + jnp.exp(-gate_pre))
        d_gate_ref[...] = (back * up_pre * sig * (1.0 + gate_pre * (1.0 - sig))).astype(jnp.bfloat16)
        d_up_ref[...] = (back * gate_pre * sig).astype(jnp.bfloat16)

    @pl.when(step >= steps)
    def _():
        total = lax.dot_general(d_gate_ref[...], gate_ref[...], ACROSS, preferred_element_type=jnp.float32)
        total += lax.dot_general(d_up_ref[...], up_ref[...], ACROSS, preferred_element_type=jnp.float32)
        out_ref[...] = total.astype(jnp.bfloat16).reshape(out_ref.shape)


def expert(arrived, w_gate, w_up, w_down, block=512):
    sources, double, width = arrived.shape
    count = double // 2
    hidden = w_gate.shape[1]
    rows = sources * count
    steps = width // block
    there = lambda j: jnp.minimum(j, steps - 1)
    back = lambda j: jnp.where(j < steps, j, 2 * steps - 1 - j)
    return pl.pallas_call(
        functools.partial(expert_body, steps=steps),
        grid=(2 * steps,),
        in_specs=[
            pl.BlockSpec((sources, double, block), lambda j: (0, 0, there(j))),
            pl.BlockSpec((block, hidden), lambda j: (back(j), 0)),
            pl.BlockSpec((block, hidden), lambda j: (back(j), 0)),
            pl.BlockSpec((hidden, block), lambda j: (0, there(j))),
        ],
        out_specs=pl.BlockSpec(
            (sources, count, block), lambda j: (0, 0, jnp.where(j < steps, steps - 1, 2 * steps - 1 - j))
        ),
        out_shape=jax.ShapeDtypeStruct((sources, count, width), jnp.bfloat16),
        scratch_shapes=[pltpu.VMEM((rows, hidden), jnp.float32)] * 3
        + [pltpu.VMEM((rows, hidden), jnp.bfloat16)] * 2,
        compiler_params=params(),
        cost_estimate=pl.CostEstimate(
            flops=10 * rows * width * hidden,
            transcendentals=rows * hidden,
            bytes_accessed=2 * (5 * width * hidden + 3 * rows * width),
        ),
        name="expert",
    )(arrived, w_gate, w_up, w_down)


def scale_of(slot, weight, first, count):
    experts, tok_rows = slot.shape
    shape = (experts, count, tok_rows)
    wanted = (first + lax.broadcasted_iota(jnp.int32, shape, 1)).astype(jnp.float32)
    hit = jnp.broadcast_to(slot[:, None, :], shape) == wanted
    scale = jnp.where(hit, jnp.broadcast_to(weight[:, None, :], shape), 0.0)
    scale = scale.reshape(experts * count, tok_rows).T
    high = scale.astype(jnp.bfloat16)
    low = (scale - high.astype(jnp.float32)).astype(jnp.bfloat16)
    return jnp.concatenate([high, low], axis=0)


def weighted(scale_ref, block_ref):
    flat = block_ref[...].reshape(scale_ref.shape[1], block_ref.shape[2])
    total = jnp.dot(scale_ref[...], flat, preferred_element_type=jnp.float32)
    tok_rows = total.shape[0] // 2
    return total[0:tok_rows] + total[tok_rows:]


def combine_a_body(ids_ref, gates_ref, block_ref, total_ref, late_ref, scale_ref, *, chunks, experts):
    topk, tok_rows = ids_ref.shape

    @pl.when(pl.program_id(0) == 0)
    def _():
        slot = slots_of(ids_ref, experts)
        numbers = lax.broadcasted_iota(jnp.int32, (experts, tok_rows), 0)
        weight = jnp.zeros((experts, tok_rows), jnp.float32)
        for k in range(topk):
            weight = jnp.where(ids_ref[k : k + 1, :] == numbers, gates_ref[k : k + 1, :], weight)
        scale_ref[...] = scale_of(slot, weight, *chunks[0])
        late_ref[...] = scale_of(slot, weight, *chunks[1])

    total_ref[...] = weighted(scale_ref, block_ref)


def combine_a(ids, gates, returned, chunks, block=896):
    topk, tok_rows = ids.shape
    experts, count, width = returned.shape
    whole = pl.BlockSpec((topk, tok_rows), lambda j: (0, 0))
    late = (2 * tok_rows, experts * chunks[1][1])
    return pl.pallas_call(
        functools.partial(combine_a_body, chunks=chunks, experts=experts),
        grid=(width // block,),
        in_specs=[whole, whole, pl.BlockSpec((experts, count, block), lambda j: (0, 0, j))],
        out_specs=[
            pl.BlockSpec((tok_rows, block), lambda j: (0, j)),
            pl.BlockSpec(late, lambda j: (0, 0)),
        ],
        out_shape=[
            jax.ShapeDtypeStruct((tok_rows, width), jnp.float32),
            jax.ShapeDtypeStruct(late, jnp.bfloat16),
        ],
        scratch_shapes=[pltpu.VMEM((2 * tok_rows, experts * count), jnp.bfloat16)],
        compiler_params=params(),
        name="combine_first",
    )(ids, gates, returned)


def combine_b_body(scale_ref, block_ref, prior_ref, out_ref):
    block = out_ref.shape[1]
    start = pl.multiple_of(pl.program_id(0) * block, 128)
    part = block_ref.at[:, :, pl.ds(start, block)]
    out_ref[...] = (prior_ref[...] + weighted(scale_ref, part)).astype(jnp.bfloat16)


def combine_b(scale, returned, prior, block=1792):
    experts, count, width = returned.shape
    tok_rows = prior.shape[0]
    part = pl.BlockSpec((tok_rows, block), lambda j: (0, j))
    return pl.pallas_call(
        combine_b_body,
        grid=(width // block,),
        in_specs=[
            pl.BlockSpec(scale.shape, lambda j: (0, 0)),
            pl.BlockSpec(memory_space=pltpu.VMEM),
            part,
        ],
        out_specs=part,
        out_shape=jax.ShapeDtypeStruct((tok_rows, width), jnp.bfloat16),
        compiler_params=params(),
        name="combine_last",
    )(scale, returned, prior)


def exchange(block):
    return lax.all_to_all(block, AXES, split_axis=0, concat_axis=0, tiled=True)


def body(tokens_in, grad_out, expert_ids, gate_weights, w_gate, w_up, w_down):
    experts = lax.axis_size("node") * lax.axis_size("local")
    ids = expert_ids.T
    gates = gate_weights.T
    (first_a, count_a), (first_b, count_b) = CHUNKS
    payload_a = pack(ids, tokens_in, grad_out, experts, first_a, count_a)
    payload_a, ids_late = lax.optimization_barrier((payload_a, ids))
    arrived_a = exchange(payload_a)
    payload_b = pack(ids_late, tokens_in, grad_out, experts, first_b, count_b)
    arrived_b = exchange(payload_b)
    result_a = expert(arrived_a, w_gate[0], w_up[0], w_down[0])
    returned_a = exchange(result_a)
    result_b = expert(arrived_b, w_gate[0], w_up[0], w_down[0])
    returned_b = exchange(result_b)
    total, scale_b = combine_a(ids, gates, returned_a, CHUNKS)
    returned_b = pltpu.with_memory_space_constraint(returned_b, pltpu.VMEM)
    return combine_b(scale_b, returned_b, total)


def solution(mesh):
    rows = P(AXES, None)
    cube = P(AXES, None, None)
    in_specs = (rows, rows, rows, rows, cube, cube, cube)
    return jax.shard_map(body, mesh=mesh, in_specs=in_specs, out_specs=rows, check_vma=False)
```

```python
import functools

import jax
import jax.numpy as jnp
from jax import lax
from jax.experimental import pallas as pl
from jax.experimental.pallas import tpu as pltpu
from jax.sharding import Mesh
from jax.sharding import PartitionSpec as P

CHIPS = (("x", 4), ("y", 4), ("core", 2), ("z", 4))
OWNERS = ("x", "y", "core", "z")
PEERS = ("y", "core", "z", "x")
CHUNKS = ((0, 4), (4, 2))
VMEM_LIMIT = 60 * 1024 * 1024
ACROSS = (((1,), (1,)), ((), ()))


def params():
    return pltpu.CompilerParams(dimension_semantics=("arbitrary",), vmem_limit_bytes=VMEM_LIMIT)


def peer_experts(experts, tok_rows):
    sizes = dict(CHIPS)
    rank = lax.broadcasted_iota(jnp.int32, (experts, tok_rows), 0)
    place = {}
    for axis in reversed(PEERS):
        place[axis] = rank % sizes[axis]
        rank = rank // sizes[axis]
    number = jnp.zeros((experts, tok_rows), jnp.int32)
    for axis in OWNERS:
        number = number * sizes[axis] + place[axis]
    return number


def slots_of(ids_ref, experts):
    topk, tok_rows = ids_ref.shape
    numbers = peer_experts(experts, tok_rows)
    member = ids_ref[0:1, :] == numbers
    for k in range(1, topk):
        member = member | (ids_ref[k : k + 1, :] == numbers)
    source = lax.broadcasted_iota(jnp.int32, (tok_rows, tok_rows), 0)
    target = lax.broadcasted_iota(jnp.int32, (tok_rows, tok_rows), 1)
    before = jnp.where(source < target, 1.0, 0.0).astype(jnp.bfloat16)
    flags = jnp.where(member, 1.0, 0.0).astype(jnp.bfloat16)
    slot = jnp.dot(flags, before, preferred_element_type=jnp.float32)
    return jnp.where(member, slot, -1.0)


def pack_body(ids_ref, x_ref, y_ref, out_ref, pick_ref, *, first, count, experts):
    tok_rows = ids_ref.shape[1]

    @pl.when(pl.program_id(0) == 0)
    def _():
        shape = (experts, 2 * count, 2 * tok_rows)
        slot = slots_of(ids_ref, experts)
        slot = jnp.concatenate([slot, slot], axis=1)
        row = lax.broadcasted_iota(jnp.int32, shape, 1)
        column = lax.broadcasted_iota(jnp.int32, shape, 2)
        wanted = (first + row % count).astype(jnp.float32)
        same = (row >= count) == (column >= tok_rows)
        hit = same & (jnp.broadcast_to(slot[:, None, :], shape) == wanted)
        picked = jnp.where(hit, 1.0, 0.0)
        pick_ref[...] = picked.reshape(experts * 2 * count, 2 * tok_rows).astype(jnp.bfloat16)

    both = jnp.concatenate([x_ref[...], y_ref[...]], axis=0)
    block = jnp.dot(pick_ref[...], both, preferred_element_type=jnp.float32)
    out_ref[...] = block.astype(jnp.bfloat16).reshape(out_ref.shape)


def pack(ids, x, y, experts, first, count, block=1792):
    topk, tok_rows = ids.shape
    width = x.shape[1]
    part = pl.BlockSpec((tok_rows, block), lambda j: (0, j))
    return pl.pallas_call(
        functools.partial(pack_body, first=first, count=count, experts=experts),
        grid=(width // block,),
        in_specs=[pl.BlockSpec((topk, tok_rows), lambda j: (0, 0)), part, part],
        out_specs=pl.BlockSpec((experts, 2 * count, block), lambda j: (0, 0, j)),
        out_shape=jax.ShapeDtypeStruct((experts, 2 * count, width), jnp.bfloat16),
        scratch_shapes=[pltpu.VMEM((experts * 2 * count, 2 * tok_rows), jnp.bfloat16)],
        compiler_params=params(),
        name="pack",
    )(ids, x, y)


def expert_body(
    in_ref, gate_ref, up_ref, down_ref, out_ref,
    gate_acc, up_acc, back_acc, d_gate_ref, d_up_ref, *, steps,
):
    step = pl.program_id(0)
    rows = gate_acc.shape[0]
    count = in_ref.shape[1] // 2
    block = in_ref.shape[2]

    def add(acc, value, start):
        if start:
            acc[...] = value
        else:
            acc[...] += value

    def forward(start):
        x = in_ref[:, 0:count, :].reshape(rows, block)
        y = in_ref[:, count : 2 * count, :].reshape(rows, block)
        add(gate_acc, jnp.dot(x, gate_ref[...], preferred_element_type=jnp.float32), start)
        add(up_acc, jnp.dot(x, up_ref[...], preferred_element_type=jnp.float32), start)
        add(back_acc, lax.dot_general(y, down_ref[...], ACROSS, preferred_element_type=jnp.float32), start)

    @pl.when(step == 0)
    def _():
        forward(True)

    @pl.when((step > 0) & (step < steps))
    def _():
        forward(False)

    @pl.when(step == steps - 1)
    def _():
        gate_pre = gate_acc[...]
        up_pre = up_acc[...]
        back = back_acc[...]
        sig = 1.0 / (1.0 + jnp.exp(-gate_pre))
        d_gate_ref[...] = (back * up_pre * sig * (1.0 + gate_pre * (1.0 - sig))).astype(jnp.bfloat16)
        d_up_ref[...] = (back * gate_pre * sig).astype(jnp.bfloat16)

    @pl.when(step >= steps)
    def _():
        total = lax.dot_general(d_gate_ref[...], gate_ref[...], ACROSS, preferred_element_type=jnp.float32)
        total += lax.dot_general(d_up_ref[...], up_ref[...], ACROSS, preferred_element_type=jnp.float32)
        out_ref[...] = total.astype(jnp.bfloat16).reshape(out_ref.shape)


def expert(arrived, w_gate, w_up, w_down, block=512):
    sources, double, width = arrived.shape
    count = double // 2
    hidden = w_gate.shape[1]
    rows = sources * count
    steps = width // block
    there = lambda j: jnp.minimum(j, steps - 1)
    back = lambda j: jnp.where(j < steps, j, 2 * steps - 1 - j)
    return pl.pallas_call(
        functools.partial(expert_body, steps=steps),
        grid=(2 * steps,),
        in_specs=[
            pl.BlockSpec((sources, double, block), lambda j: (0, 0, there(j))),
            pl.BlockSpec((block, hidden), lambda j: (back(j), 0)),
            pl.BlockSpec((block, hidden), lambda j: (back(j), 0)),
            pl.BlockSpec((hidden, block), lambda j: (0, there(j))),
        ],
        out_specs=pl.BlockSpec(
            (sources, count, block), lambda j: (0, 0, jnp.where(j < steps, steps - 1, 2 * steps - 1 - j))
        ),
        out_shape=jax.ShapeDtypeStruct((sources, count, width), jnp.bfloat16),
        scratch_shapes=[pltpu.VMEM((rows, hidden), jnp.float32)] * 3
        + [pltpu.VMEM((rows, hidden), jnp.bfloat16)] * 2,
        compiler_params=params(),
        cost_estimate=pl.CostEstimate(
            flops=10 * rows * width * hidden,
            transcendentals=rows * hidden,
            bytes_accessed=2 * (5 * width * hidden + 3 * rows * width),
        ),
        name="expert",
    )(arrived, w_gate, w_up, w_down)


def scale_of(slot, weight, first, count):
    experts, tok_rows = slot.shape
    shape = (experts, count, tok_rows)
    wanted = (first + lax.broadcasted_iota(jnp.int32, shape, 1)).astype(jnp.float32)
    hit = jnp.broadcast_to(slot[:, None, :], shape) == wanted
    scale = jnp.where(hit, jnp.broadcast_to(weight[:, None, :], shape), 0.0)
    scale = scale.reshape(experts * count, tok_rows).T
    high = scale.astype(jnp.bfloat16)
    low = (scale - high.astype(jnp.float32)).astype(jnp.bfloat16)
    return jnp.concatenate([high, low], axis=0)


def weighted(scale_ref, block_ref):
    flat = block_ref[...].reshape(scale_ref.shape[1], block_ref.shape[2])
    total = jnp.dot(scale_ref[...], flat, preferred_element_type=jnp.float32)
    tok_rows = total.shape[0] // 2
    return total[0:tok_rows] + total[tok_rows:]


def combine_a_body(ids_ref, gates_ref, block_ref, total_ref, late_ref, scale_ref, *, chunks, experts):
    topk, tok_rows = ids_ref.shape

    @pl.when(pl.program_id(0) == 0)
    def _():
        slot = slots_of(ids_ref, experts)
        numbers = peer_experts(experts, tok_rows)
        weight = jnp.zeros((experts, tok_rows), jnp.float32)
        for k in range(topk):
            weight = jnp.where(ids_ref[k : k + 1, :] == numbers, gates_ref[k : k + 1, :], weight)
        scale_ref[...] = scale_of(slot, weight, *chunks[0])
        late_ref[...] = scale_of(slot, weight, *chunks[1])

    total_ref[...] = weighted(scale_ref, block_ref)


def combine_a(ids, gates, returned, chunks, block=896):
    topk, tok_rows = ids.shape
    experts, count, width = returned.shape
    whole = pl.BlockSpec((topk, tok_rows), lambda j: (0, 0))
    late = (2 * tok_rows, experts * chunks[1][1])
    return pl.pallas_call(
        functools.partial(combine_a_body, chunks=chunks, experts=experts),
        grid=(width // block,),
        in_specs=[whole, whole, pl.BlockSpec((experts, count, block), lambda j: (0, 0, j))],
        out_specs=[
            pl.BlockSpec((tok_rows, block), lambda j: (0, j)),
            pl.BlockSpec(late, lambda j: (0, 0)),
        ],
        out_shape=[
            jax.ShapeDtypeStruct((tok_rows, width), jnp.float32),
            jax.ShapeDtypeStruct(late, jnp.bfloat16),
        ],
        scratch_shapes=[pltpu.VMEM((2 * tok_rows, experts * count), jnp.bfloat16)],
        compiler_params=params(),
        name="combine_first",
    )(ids, gates, returned)


def combine_b_body(scale_ref, block_ref, prior_ref, out_ref):
    block = out_ref.shape[1]
    start = pl.multiple_of(pl.program_id(0) * block, 128)
    part = block_ref.at[:, :, pl.ds(start, block)]
    out_ref[...] = (prior_ref[...] + weighted(scale_ref, part)).astype(jnp.bfloat16)


def combine_b(scale, returned, prior, block=1792):
    experts, count, width = returned.shape
    tok_rows = prior.shape[0]
    part = pl.BlockSpec((tok_rows, block), lambda j: (0, j))
    return pl.pallas_call(
        combine_b_body,
        grid=(width // block,),
        in_specs=[
            pl.BlockSpec(scale.shape, lambda j: (0, 0)),
            pl.BlockSpec(memory_space=pltpu.VMEM),
            part,
        ],
        out_specs=part,
        out_shape=jax.ShapeDtypeStruct((tok_rows, width), jnp.bfloat16),
        compiler_params=params(),
        name="combine_last",
    )(scale, returned, prior)


def exchange(block):
    return lax.all_to_all(block, PEERS, split_axis=0, concat_axis=0, tiled=True)


def body(tokens_in, grad_out, expert_ids, gate_weights, w_gate, w_up, w_down):
    experts = lax.axis_size(PEERS)
    ids = expert_ids.T
    gates = gate_weights.T
    (first_a, count_a), (first_b, count_b) = CHUNKS
    payload_a = pack(ids, tokens_in, grad_out, experts, first_a, count_a)
    payload_a, ids_late = lax.optimization_barrier((payload_a, ids))
    arrived_a = exchange(payload_a)
    payload_b = pack(ids_late, tokens_in, grad_out, experts, first_b, count_b)
    arrived_b = exchange(payload_b)
    result_a = expert(arrived_a, w_gate[0], w_up[0], w_down[0])
    returned_a = exchange(result_a)
    result_b = expert(arrived_b, w_gate[0], w_up[0], w_down[0])
    returned_b = exchange(result_b)
    total, scale_b = combine_a(ids, gates, returned_a, CHUNKS)
    returned_b = pltpu.with_memory_space_constraint(returned_b, pltpu.VMEM)
    return combine_b(scale_b, returned_b, total)


def solution(mesh):
    sizes = tuple(size for _, size in CHIPS)
    chips = Mesh(mesh.devices.reshape(sizes), OWNERS)
    rows = P(OWNERS, None)
    cube = P(OWNERS, None, None)
    in_specs = (rows, rows, rows, rows, cube, cube, cube)
    return jax.shard_map(body, mesh=chips, in_specs=in_specs, out_specs=rows, check_vma=False)
```

```python
import functools

import jax
import jax.numpy as jnp
from jax import lax
from jax.experimental import pallas as pl
from jax.experimental.pallas import tpu as pltpu
from jax.sharding import Mesh
from jax.sharding import PartitionSpec as P

CHIPS = (("x", 4), ("y", 4), ("core", 2), ("z", 4))
OWNERS = ("x", "y", "core", "z")
PEERS = ("z", "core", "x", "y")
CHUNKS = ((0, 4), (4, 2))
VMEM_LIMIT = 60 * 1024 * 1024
ACROSS = (((1,), (1,)), ((), ()))


def params():
    return pltpu.CompilerParams(dimension_semantics=("arbitrary",), vmem_limit_bytes=VMEM_LIMIT)


def peer_experts(experts, tok_rows):
    sizes = dict(CHIPS)
    rank = lax.broadcasted_iota(jnp.int32, (experts, tok_rows), 0)
    place = {}
    for axis in reversed(PEERS):
        place[axis] = rank % sizes[axis]
        rank = rank // sizes[axis]
    number = jnp.zeros((experts, tok_rows), jnp.int32)
    for axis in OWNERS:
        number = number * sizes[axis] + place[axis]
    return number


def slots_of(ids_ref, experts):
    topk, tok_rows = ids_ref.shape
    numbers = peer_experts(experts, tok_rows)
    member = ids_ref[0:1, :] == numbers
    for k in range(1, topk):
        member = member | (ids_ref[k : k + 1, :] == numbers)
    source = lax.broadcasted_iota(jnp.int32, (tok_rows, tok_rows), 0)
    target = lax.broadcasted_iota(jnp.int32, (tok_rows, tok_rows), 1)
    before = jnp.where(source < target, 1.0, 0.0).astype(jnp.bfloat16)
    flags = jnp.where(member, 1.0, 0.0).astype(jnp.bfloat16)
    slot = jnp.dot(flags, before, preferred_element_type=jnp.float32)
    return jnp.where(member, slot, -1.0)


def pack_body(ids_ref, x_ref, y_ref, out_ref, pick_ref, *, first, count, experts):
    tok_rows = ids_ref.shape[1]

    @pl.when(pl.program_id(0) == 0)
    def _():
        shape = (experts, 2 * count, 2 * tok_rows)
        slot = slots_of(ids_ref, experts)
        slot = jnp.concatenate([slot, slot], axis=1)
        row = lax.broadcasted_iota(jnp.int32, shape, 1)
        column = lax.broadcasted_iota(jnp.int32, shape, 2)
        wanted = (first + row % count).astype(jnp.float32)
        same = (row >= count) == (column >= tok_rows)
        hit = same & (jnp.broadcast_to(slot[:, None, :], shape) == wanted)
        picked = jnp.where(hit, 1.0, 0.0)
        pick_ref[...] = picked.reshape(experts * 2 * count, 2 * tok_rows).astype(jnp.bfloat16)

    both = jnp.concatenate([x_ref[...], y_ref[...]], axis=0)
    block = jnp.dot(pick_ref[...], both, preferred_element_type=jnp.float32)
    out_ref[...] = block.astype(jnp.bfloat16).reshape(out_ref.shape)


def pack(ids, x, y, experts, first, count, block=1792):
    topk, tok_rows = ids.shape
    width = x.shape[1]
    part = pl.BlockSpec((tok_rows, block), lambda j: (0, j))
    return pl.pallas_call(
        functools.partial(pack_body, first=first, count=count, experts=experts),
        grid=(width // block,),
        in_specs=[pl.BlockSpec((topk, tok_rows), lambda j: (0, 0)), part, part],
        out_specs=pl.BlockSpec((experts, 2 * count, block), lambda j: (0, 0, j)),
        out_shape=jax.ShapeDtypeStruct((experts, 2 * count, width), jnp.bfloat16),
        scratch_shapes=[pltpu.VMEM((experts * 2 * count, 2 * tok_rows), jnp.bfloat16)],
        compiler_params=params(),
        name="pack",
    )(ids, x, y)


def expert_body(
    in_ref, gate_ref, up_ref, down_ref, out_ref,
    gate_acc, up_acc, back_acc, d_gate_ref, d_up_ref, *, steps,
):
    step = pl.program_id(0)
    rows = gate_acc.shape[0]
    count = in_ref.shape[1] // 2
    block = in_ref.shape[2]

    def add(acc, value, start):
        if start:
            acc[...] = value
        else:
            acc[...] += value

    def forward(start):
        x = in_ref[:, 0:count, :].reshape(rows, block)
        y = in_ref[:, count : 2 * count, :].reshape(rows, block)
        add(gate_acc, jnp.dot(x, gate_ref[...], preferred_element_type=jnp.float32), start)
        add(up_acc, jnp.dot(x, up_ref[...], preferred_element_type=jnp.float32), start)
        add(back_acc, lax.dot_general(y, down_ref[...], ACROSS, preferred_element_type=jnp.float32), start)

    @pl.when(step == 0)
    def _():
        forward(True)

    @pl.when((step > 0) & (step < steps))
    def _():
        forward(False)

    @pl.when(step == steps - 1)
    def _():
        gate_pre = gate_acc[...]
        up_pre = up_acc[...]
        back = back_acc[...]
        sig = 1.0 / (1.0 + jnp.exp(-gate_pre))
        d_gate_ref[...] = (back * up_pre * sig * (1.0 + gate_pre * (1.0 - sig))).astype(jnp.bfloat16)
        d_up_ref[...] = (back * gate_pre * sig).astype(jnp.bfloat16)

    @pl.when(step >= steps)
    def _():
        total = lax.dot_general(d_gate_ref[...], gate_ref[...], ACROSS, preferred_element_type=jnp.float32)
        total += lax.dot_general(d_up_ref[...], up_ref[...], ACROSS, preferred_element_type=jnp.float32)
        out_ref[...] = total.astype(jnp.bfloat16).reshape(out_ref.shape)


def expert(arrived, w_gate, w_up, w_down, block=512):
    sources, double, width = arrived.shape
    count = double // 2
    hidden = w_gate.shape[1]
    rows = sources * count
    steps = width // block
    there = lambda j: jnp.minimum(j, steps - 1)
    back = lambda j: jnp.where(j < steps, j, 2 * steps - 1 - j)
    return pl.pallas_call(
        functools.partial(expert_body, steps=steps),
        grid=(2 * steps,),
        in_specs=[
            pl.BlockSpec((sources, double, block), lambda j: (0, 0, there(j))),
            pl.BlockSpec((block, hidden), lambda j: (back(j), 0)),
            pl.BlockSpec((block, hidden), lambda j: (back(j), 0)),
            pl.BlockSpec((hidden, block), lambda j: (0, there(j))),
        ],
        out_specs=pl.BlockSpec(
            (sources, count, block), lambda j: (0, 0, jnp.where(j < steps, steps - 1, 2 * steps - 1 - j))
        ),
        out_shape=jax.ShapeDtypeStruct((sources, count, width), jnp.bfloat16),
        scratch_shapes=[pltpu.VMEM((rows, hidden), jnp.float32)] * 3
        + [pltpu.VMEM((rows, hidden), jnp.bfloat16)] * 2,
        compiler_params=params(),
        cost_estimate=pl.CostEstimate(
            flops=10 * rows * width * hidden,
            transcendentals=rows * hidden,
            bytes_accessed=2 * (5 * width * hidden + 3 * rows * width),
        ),
        name="expert",
    )(arrived, w_gate, w_up, w_down)


def scale_of(slot, weight, first, count):
    experts, tok_rows = slot.shape
    shape = (experts, count, tok_rows)
    wanted = (first + lax.broadcasted_iota(jnp.int32, shape, 1)).astype(jnp.float32)
    hit = jnp.broadcast_to(slot[:, None, :], shape) == wanted
    scale = jnp.where(hit, jnp.broadcast_to(weight[:, None, :], shape), 0.0)
    scale = scale.reshape(experts * count, tok_rows).T
    high = scale.astype(jnp.bfloat16)
    low = (scale - high.astype(jnp.float32)).astype(jnp.bfloat16)
    return jnp.concatenate([high, low], axis=0)


def weighted(scale_ref, block_ref):
    flat = block_ref[...].reshape(scale_ref.shape[1], block_ref.shape[2])
    total = jnp.dot(scale_ref[...], flat, preferred_element_type=jnp.float32)
    tok_rows = total.shape[0] // 2
    return total[0:tok_rows] + total[tok_rows:]


def combine_a_body(ids_ref, gates_ref, block_ref, total_ref, late_ref, scale_ref, *, chunks, experts):
    topk, tok_rows = ids_ref.shape

    @pl.when(pl.program_id(0) == 0)
    def _():
        slot = slots_of(ids_ref, experts)
        numbers = peer_experts(experts, tok_rows)
        weight = jnp.zeros((experts, tok_rows), jnp.float32)
        for k in range(topk):
            weight = jnp.where(ids_ref[k : k + 1, :] == numbers, gates_ref[k : k + 1, :], weight)
        scale_ref[...] = scale_of(slot, weight, *chunks[0])
        late_ref[...] = scale_of(slot, weight, *chunks[1])

    total_ref[...] = weighted(scale_ref, block_ref)


def combine_a(ids, gates, returned, chunks, block=896):
    topk, tok_rows = ids.shape
    experts, count, width = returned.shape
    whole = pl.BlockSpec((topk, tok_rows), lambda j: (0, 0))
    late = (2 * tok_rows, experts * chunks[1][1])
    return pl.pallas_call(
        functools.partial(combine_a_body, chunks=chunks, experts=experts),
        grid=(width // block,),
        in_specs=[whole, whole, pl.BlockSpec((experts, count, block), lambda j: (0, 0, j))],
        out_specs=[
            pl.BlockSpec((tok_rows, block), lambda j: (0, j)),
            pl.BlockSpec(late, lambda j: (0, 0)),
        ],
        out_shape=[
            jax.ShapeDtypeStruct((tok_rows, width), jnp.float32),
            jax.ShapeDtypeStruct(late, jnp.bfloat16),
        ],
        scratch_shapes=[pltpu.VMEM((2 * tok_rows, experts * count), jnp.bfloat16)],
        compiler_params=params(),
        name="combine_first",
    )(ids, gates, returned)


def combine_b_body(scale_ref, block_ref, prior_ref, out_ref):
    block = out_ref.shape[1]
    start = pl.multiple_of(pl.program_id(0) * block, 128)
    part = block_ref.at[:, :, pl.ds(start, block)]
    out_ref[...] = (prior_ref[...] + weighted(scale_ref, part)).astype(jnp.bfloat16)


def combine_b(scale, returned, prior, block=1792):
    experts, count, width = returned.shape
    tok_rows = prior.shape[0]
    part = pl.BlockSpec((tok_rows, block), lambda j: (0, j))
    return pl.pallas_call(
        combine_b_body,
        grid=(width // block,),
        in_specs=[
            pl.BlockSpec(scale.shape, lambda j: (0, 0)),
            pl.BlockSpec(memory_space=pltpu.VMEM),
            part,
        ],
        out_specs=part,
        out_shape=jax.ShapeDtypeStruct((tok_rows, width), jnp.bfloat16),
        compiler_params=params(),
        name="combine_last",
    )(scale, returned, prior)


def exchange(block):
    return lax.all_to_all(block, PEERS, split_axis=0, concat_axis=0, tiled=True)


def body(tokens_in, grad_out, expert_ids, gate_weights, w_gate, w_up, w_down):
    experts = lax.axis_size(PEERS)
    ids = expert_ids.T
    gates = gate_weights.T
    (first_a, count_a), (first_b, count_b) = CHUNKS
    payload_a = pack(ids, tokens_in, grad_out, experts, first_a, count_a)
    payload_a, ids_late = lax.optimization_barrier((payload_a, ids))
    arrived_a = exchange(payload_a)
    payload_b = pack(ids_late, tokens_in, grad_out, experts, first_b, count_b)
    arrived_b = exchange(payload_b)
    result_a = expert(arrived_a, w_gate[0], w_up[0], w_down[0])
    returned_a = exchange(result_a)
    result_b = expert(arrived_b, w_gate[0], w_up[0], w_down[0])
    returned_b = exchange(result_b)
    total, scale_b = combine_a(ids, gates, returned_a, CHUNKS)
    returned_b = pltpu.with_memory_space_constraint(returned_b, pltpu.VMEM)
    return combine_b(scale_b, returned_b, total)


def solution(mesh):
    sizes = tuple(size for _, size in CHIPS)
    chips = Mesh(mesh.devices.reshape(sizes), OWNERS)
    rows = P(OWNERS, None)
    cube = P(OWNERS, None, None)
    in_specs = (rows, rows, rows, rows, cube, cube, cube)
    return jax.shard_map(body, mesh=chips, in_specs=in_specs, out_specs=rows, check_vma=False)
```

```python
import functools

import jax
import jax.numpy as jnp
from jax import lax
from jax.experimental import pallas as pl
from jax.experimental.pallas import tpu as pltpu
from jax.sharding import Mesh
from jax.sharding import PartitionSpec as P

CHIPS = (("x", 4), ("y", 4), ("core", 2), ("z", 4))
OWNERS = ("x", "y", "core", "z")
PEERS = ("z", "core", "x", "y")
CHUNKS = ((0, 4), (4, 2))
VMEM_LIMIT = 60 * 1024 * 1024
ACROSS = (((1,), (1,)), ((), ()))


def params(limit=VMEM_LIMIT):
    return pltpu.CompilerParams(dimension_semantics=("arbitrary",), vmem_limit_bytes=limit)


def peer_experts(experts, tok_rows):
    sizes = dict(CHIPS)
    rank = lax.broadcasted_iota(jnp.int32, (experts, tok_rows), 0)
    place = {}
    for axis in reversed(PEERS):
        place[axis] = rank % sizes[axis]
        rank = rank // sizes[axis]
    number = jnp.zeros((experts, tok_rows), jnp.int32)
    for axis in OWNERS:
        number = number * sizes[axis] + place[axis]
    return number


def slots_of(ids_ref, experts):
    topk, tok_rows = ids_ref.shape
    numbers = peer_experts(experts, tok_rows)
    member = ids_ref[0:1, :] == numbers
    for k in range(1, topk):
        member = member | (ids_ref[k : k + 1, :] == numbers)
    source = lax.broadcasted_iota(jnp.int32, (tok_rows, tok_rows), 0)
    target = lax.broadcasted_iota(jnp.int32, (tok_rows, tok_rows), 1)
    before = jnp.where(source < target, 1.0, 0.0).astype(jnp.bfloat16)
    flags = jnp.where(member, 1.0, 0.0).astype(jnp.bfloat16)
    slot = jnp.dot(flags, before, preferred_element_type=jnp.float32)
    return jnp.where(member, slot, -1.0)


def pack_body(ids_ref, x_ref, y_ref, out_ref, pick_ref, *, first, count, experts):
    tok_rows = ids_ref.shape[1]

    @pl.when(pl.program_id(0) == 0)
    def _():
        shape = (experts, 2 * count, 2 * tok_rows)
        slot = slots_of(ids_ref, experts)
        slot = jnp.concatenate([slot, slot], axis=1)
        row = lax.broadcasted_iota(jnp.int32, shape, 1)
        column = lax.broadcasted_iota(jnp.int32, shape, 2)
        wanted = (first + row % count).astype(jnp.float32)
        same = (row >= count) == (column >= tok_rows)
        hit = same & (jnp.broadcast_to(slot[:, None, :], shape) == wanted)
        picked = jnp.where(hit, 1.0, 0.0)
        pick_ref[...] = picked.reshape(experts * 2 * count, 2 * tok_rows).astype(jnp.bfloat16)

    both = jnp.concatenate([x_ref[...], y_ref[...]], axis=0)
    block = jnp.dot(pick_ref[...], both, preferred_element_type=jnp.float32)
    out_ref[...] = block.astype(jnp.bfloat16).reshape(out_ref.shape)


def pack(ids, x, y, experts, first, count, block=1792):
    topk, tok_rows = ids.shape
    width = x.shape[1]
    part = pl.BlockSpec((tok_rows, block), lambda j: (0, j))
    return pl.pallas_call(
        functools.partial(pack_body, first=first, count=count, experts=experts),
        grid=(width // block,),
        in_specs=[pl.BlockSpec((topk, tok_rows), lambda j: (0, 0)), part, part],
        out_specs=pl.BlockSpec((experts, 2 * count, block), lambda j: (0, 0, j)),
        out_shape=jax.ShapeDtypeStruct((experts, 2 * count, width), jnp.bfloat16),
        scratch_shapes=[pltpu.VMEM((experts * 2 * count, 2 * tok_rows), jnp.bfloat16)],
        compiler_params=params(),
        name="pack",
    )(ids, x, y)


def expert_body(
    in_ref, gate_ref, up_ref, down_ref, out_ref,
    gate_acc, up_acc, back_acc, d_gate_ref, d_up_ref, *, steps,
):
    step = pl.program_id(0)
    rows = gate_acc.shape[0]
    count = in_ref.shape[1] // 2
    block = in_ref.shape[2]

    def add(acc, value, start):
        if start:
            acc[...] = value
        else:
            acc[...] += value

    def forward(start):
        x = in_ref[:, 0:count, :].reshape(rows, block)
        y = in_ref[:, count : 2 * count, :].reshape(rows, block)
        add(gate_acc, jnp.dot(x, gate_ref[...], preferred_element_type=jnp.float32), start)
        add(up_acc, jnp.dot(x, up_ref[...], preferred_element_type=jnp.float32), start)
        add(back_acc, lax.dot_general(y, down_ref[...], ACROSS, preferred_element_type=jnp.float32), start)

    @pl.when(step == 0)
    def _():
        forward(True)

    @pl.when((step > 0) & (step < steps))
    def _():
        forward(False)

    @pl.when(step == steps - 1)
    def _():
        gate_pre = gate_acc[...]
        up_pre = up_acc[...]
        back = back_acc[...]
        sig = 1.0 / (1.0 + jnp.exp(-gate_pre))
        d_gate_ref[...] = (back * up_pre * sig * (1.0 + gate_pre * (1.0 - sig))).astype(jnp.bfloat16)
        d_up_ref[...] = (back * gate_pre * sig).astype(jnp.bfloat16)

    @pl.when(step >= steps)
    def _():
        total = lax.dot_general(d_gate_ref[...], gate_ref[...], ACROSS, preferred_element_type=jnp.float32)
        total += lax.dot_general(d_up_ref[...], up_ref[...], ACROSS, preferred_element_type=jnp.float32)
        out_ref[...] = total.astype(jnp.bfloat16).reshape(out_ref.shape)


def expert(arrived, w_gate, w_up, w_down, block=512):
    sources, double, width = arrived.shape
    count = double // 2
    hidden = w_gate.shape[1]
    rows = sources * count
    steps = width // block
    there = lambda j: jnp.minimum(j, steps - 1)
    back = lambda j: jnp.where(j < steps, j, 2 * steps - 1 - j)
    return pl.pallas_call(
        functools.partial(expert_body, steps=steps),
        grid=(2 * steps,),
        in_specs=[
            pl.BlockSpec((sources, double, block), lambda j: (0, 0, there(j))),
            pl.BlockSpec((block, hidden), lambda j: (back(j), 0)),
            pl.BlockSpec((block, hidden), lambda j: (back(j), 0)),
            pl.BlockSpec((hidden, block), lambda j: (0, there(j))),
        ],
        out_specs=pl.BlockSpec(
            (sources, count, block), lambda j: (0, 0, jnp.where(j < steps, steps - 1, 2 * steps - 1 - j))
        ),
        out_shape=jax.ShapeDtypeStruct((sources, count, width), jnp.bfloat16),
        scratch_shapes=[pltpu.VMEM((rows, hidden), jnp.float32)] * 3
        + [pltpu.VMEM((rows, hidden), jnp.bfloat16)] * 2,
        compiler_params=params(),
        cost_estimate=pl.CostEstimate(
            flops=10 * rows * width * hidden,
            transcendentals=rows * hidden,
            bytes_accessed=2 * (5 * width * hidden + 3 * rows * width),
        ),
        name="expert",
    )(arrived, w_gate, w_up, w_down)


def scale_of(slot, weight, first, count):
    experts, tok_rows = slot.shape
    shape = (experts, count, tok_rows)
    wanted = (first + lax.broadcasted_iota(jnp.int32, shape, 1)).astype(jnp.float32)
    hit = jnp.broadcast_to(slot[:, None, :], shape) == wanted
    scale = jnp.where(hit, jnp.broadcast_to(weight[:, None, :], shape), 0.0)
    scale = scale.reshape(experts * count, tok_rows).T
    high = scale.astype(jnp.bfloat16)
    low = (scale - high.astype(jnp.float32)).astype(jnp.bfloat16)
    return jnp.concatenate([high, low], axis=0)


def weighted(scale_ref, block_ref):
    flat = block_ref[...].reshape(scale_ref.shape[1], block_ref.shape[2])
    total = jnp.dot(scale_ref[...], flat, preferred_element_type=jnp.float32)
    tok_rows = total.shape[0] // 2
    return total[0:tok_rows] + total[tok_rows:]


def combine_a_body(ids_ref, gates_ref, block_ref, total_ref, late_ref, scale_ref, *, chunks, experts):
    topk, tok_rows = ids_ref.shape

    @pl.when(pl.program_id(0) == 0)
    def _():
        slot = slots_of(ids_ref, experts)
        numbers = peer_experts(experts, tok_rows)
        weight = jnp.zeros((experts, tok_rows), jnp.float32)
        for k in range(topk):
            weight = jnp.where(ids_ref[k : k + 1, :] == numbers, gates_ref[k : k + 1, :], weight)
        scale_ref[...] = scale_of(slot, weight, *chunks[0])
        late_ref[...] = scale_of(slot, weight, *chunks[1])

    total_ref[...] = weighted(scale_ref, block_ref)


def combine_a(ids, gates, returned, chunks, block=896):
    topk, tok_rows = ids.shape
    experts, count, width = returned.shape
    whole = pl.BlockSpec((topk, tok_rows), lambda j: (0, 0))
    late = (2 * tok_rows, experts * chunks[1][1])
    return pl.pallas_call(
        functools.partial(combine_a_body, chunks=chunks, experts=experts),
        grid=(width // block,),
        in_specs=[whole, whole, pl.BlockSpec((experts, count, block), lambda j: (0, 0, j))],
        out_specs=[
            pl.BlockSpec((tok_rows, block), lambda j: (0, j)),
            pl.BlockSpec(late, lambda j: (0, 0)),
        ],
        out_shape=[
            jax.ShapeDtypeStruct((tok_rows, width), jnp.float32),
            jax.ShapeDtypeStruct(late, jnp.bfloat16),
        ],
        scratch_shapes=[pltpu.VMEM((2 * tok_rows, experts * count), jnp.bfloat16)],
        compiler_params=params(20 * 1024 * 1024),
        name="combine_first",
    )(ids, gates, returned)


def combine_b_body(scale_ref, block_ref, prior_ref, out_ref):
    block = out_ref.shape[1]
    start = pl.multiple_of(pl.program_id(0) * block, 128)
    part = block_ref.at[:, :, pl.ds(start, block)]
    out_ref[...] = (prior_ref[...] + weighted(scale_ref, part)).astype(jnp.bfloat16)


def combine_b(scale, returned, prior, block=1792):
    experts, count, width = returned.shape
    tok_rows = prior.shape[0]
    part = pl.BlockSpec((tok_rows, block), lambda j: (0, j))
    return pl.pallas_call(
        combine_b_body,
        grid=(width // block,),
        in_specs=[
            pl.BlockSpec(scale.shape, lambda j: (0, 0)),
            pl.BlockSpec(memory_space=pltpu.VMEM),
            part,
        ],
        out_specs=part,
        out_shape=jax.ShapeDtypeStruct((tok_rows, width), jnp.bfloat16),
        compiler_params=params(20 * 1024 * 1024),
        name="combine_last",
    )(scale, returned, prior)


def exchange(block):
    return lax.all_to_all(block, PEERS, split_axis=0, concat_axis=0, tiled=True)


def body(tokens_in, grad_out, expert_ids, gate_weights, w_gate, w_up, w_down):
    experts = lax.axis_size(PEERS)
    ids = expert_ids.T
    gates = gate_weights.T
    (first_a, count_a), (first_b, count_b) = CHUNKS
    payload_a = pack(ids, tokens_in, grad_out, experts, first_a, count_a)
    payload_a, ids_late = lax.optimization_barrier((payload_a, ids))
    arrived_a = exchange(payload_a)
    payload_b = pack(ids_late, tokens_in, grad_out, experts, first_b, count_b)
    arrived_b = exchange(payload_b)
    result_a = expert(arrived_a, w_gate[0], w_up[0], w_down[0])
    returned_a = exchange(result_a)
    result_b = expert(arrived_b, w_gate[0], w_up[0], w_down[0])
    returned_b = exchange(result_b)
    total, scale_b = combine_a(ids, gates, returned_a, CHUNKS)
    returned_b = pltpu.with_memory_space_constraint(returned_b, pltpu.VMEM)
    return combine_b(scale_b, returned_b, total)


def solution(mesh):
    sizes = tuple(size for _, size in CHIPS)
    chips = Mesh(mesh.devices.reshape(sizes), OWNERS)
    rows = P(OWNERS, None)
    cube = P(OWNERS, None, None)
    in_specs = (rows, rows, rows, rows, cube, cube, cube)
    return jax.shard_map(body, mesh=chips, in_specs=in_specs, out_specs=rows, check_vma=False)
```
